32 devices in a mesh: echo: 2 (over x), coil: 8 (over z, core), read: 2 (over y).
Axes of the slice: x: 2, y: 2, z: 4, core: 2. Of those that a mesh axis runs over, the one named last changes fastest.
Arguments:
- kspace: bfloat16 [384, 2, 8, 4, 2, 192], P(None, 'echo', 'coil', 'read'), may hold values from -3 to 3
- sampling: int32 [384, 2, 192], P(None, 'echo'), may hold values 0 or 1
- coil_maps: bfloat16 [384, 8, 4, 2, 192], P(None, 'coil', 'read'), may hold values from -1.5 to 1.5
- image: float32 [384, 2, 4, 2, 192], P('coil', 'echo', 'read'), may hold values from -6 to 6
- filters: bfloat16 [48, 3, 3, 3, 2], replicated, may hold values from -0.875 to 0.875
- thresholds: float32 [48], replicated, may hold values from 0.5 to 8
- dc_weight: float32 [2], P('echo'), may hold values from 0.5 to 2
Outputs:
- updated: float32 [384, 2, 4, 2, 192], P('coil', 'echo', 'read')
The draws below stay inside these ranges and needn't reach their ends.
All inputs are finite; a program needn't handle non-finite values. No bound on the sum of `sampling` on one device may be relied on, other than what follows from the above.
Results may differ from the reference program's by a relative error of at most 0.0033.
Values may be sent and summed in bfloat16 or wider, within the bound.
A program may use at most 128 MiB of HBM per device.

```python
import math
import jax
import jax.numpy as jnp
from jax import lax

NY = 384
NZ = 192
FILTERS = 48
ECHOES = 2
COILS = 8
RO = 4


def plant(values, rng, low, high):
    extent = values.shape
    index_at = [jax.random.randint(jax.random.fold_in(rng, axis), (), 0, extent[axis]) for axis in range(len(extent))]
    values = values.at[tuple(index_at)].set(low)
    longest = extent.index(max(extent))
    index_at[longest] = (index_at[longest] + 1) % extent[longest]
    return values.at[tuple(index_at)].set(high)


def shard_levels(rng, dims, shards, smallest, largest):
    def one(axis_at, shards_of):
        steps = jax.random.uniform(jax.random.fold_in(jax.random.fold_in(rng, 6), axis_at), (shards_of,), jnp.float32, smallest / len(shards), largest / len(shards))
        return jnp.repeat(jnp.exp(steps), dims[axis_at] // shards_of).reshape((-1,) + (1,) * (len(dims) - axis_at - 1))

    factor_of = one(*shards[0])
    for cut in shards[1:]:
        factor_of = factor_of * one(*cut)
    return factor_of


def noise(key, dims, scale, reach, cuts=(), held_as=jnp.bfloat16):
    drawn = scale * jax.random.normal(key, dims, jnp.float32)
    if cuts:
        drawn = drawn * shard_levels(key, dims, cuts, -0.22, 0.18)
    return jnp.clip(drawn, -reach, reach).astype(held_as)


def setup_inputs(seed: int = 0) -> dict:
    keys = jax.random.split(jax.random.key(seed), 8)
    kspace = noise(keys[0], (NY, ECHOES, COILS, RO, 2, NZ), 0.5, 3.0, ((1, 2), (2, 8), (3, 2)))
    sampling = plant((jax.random.randint(keys[1], (NY, ECHOES, NZ), 0, 3) < 1).astype(jnp.int32), jax.random.fold_in(keys[1], 1), 0, 1)
    coil_maps = noise(keys[2], (NY, COILS, RO, 2, NZ), 0.25, 1.5, ((1, 8), (2, 2)))
    image = noise(keys[3], (NY, ECHOES, RO, 2, NZ), 1.0, 6.0, ((0, 8), (1, 2), (2, 2)), jnp.float32)
    filters = noise(keys[4], (FILTERS, 3, 3, 3, 2), 54 ** -0.5, 0.875)
    thresholds = jnp.clip(jnp.exp(jax.random.uniform(keys[5], (FILTERS,), jnp.float32, math.log(0.5), math.log(8.0))), 0.5, 8.0)
    dc_weight = jnp.clip(jnp.exp(math.log(2.0) - 1.3862944 * jax.random.uniform(keys[6], (ECHOES,), jnp.float32) ** shard_levels(keys[6], (ECHOES,), ((0, 2),), -0.2, 0.2)), 0.5, 2.0)
    return {"kspace": kspace, "sampling": sampling, "coil_maps": coil_maps, "image": image, "filters": filters, "thresholds": thresholds, "dc_weight": dc_weight}


def tables(length):
    positions = jnp.arange(length, dtype=jnp.int32)
    product = positions[:, None] * positions[None, :] % length
    phases = product.astype(jnp.float32) * (2.0 * jnp.pi / length)
    normalize = length ** (-0.5)
    return (jnp.cos(phases) * normalize, jnp.sin(phases) * normalize)

def complex_times(left, right, conjugate):
    left_real = left[..., 0, :]
    left_imag = left[..., 1, :]
    right_real = right[..., 0, :]
    right_imag = right[..., 1, :]
    if conjugate:
        return jnp.stack([left_real * right_real + left_imag * right_imag, left_real * right_imag - left_imag * right_real], -2)
    return jnp.stack([left_real * right_real - left_imag * right_imag, left_real * right_imag + left_imag * right_real], -2)

def column_section(values, block):
    shape = values.shape
    merged = values.reshape(shape[:-2] + (shape[-2] * shape[-1],)).astype(jnp.float32)
    result = jnp.dot(merged, block.astype(jnp.float32))
    return result.reshape(shape)

def row_section(values, row_table, adjoint):
    lines = values.shape[0]
    result = jnp.einsum('ay,y...->a...', row_table.astype(jnp.float32), values.astype(jnp.float32))
    cosine_part = result[:lines]
    sine_part = result[lines:]
    if adjoint:
        return jnp.stack([cosine_part[..., 0, :] - sine_part[..., 1, :], cosine_part[..., 1, :] + sine_part[..., 0, :]], -2)
    return jnp.stack([cosine_part[..., 0, :] + sine_part[..., 1, :], cosine_part[..., 1, :] - sine_part[..., 0, :]], -2)

def reference(kspace, sampling, coil_maps, image, filters, thresholds, dc_weight):
    row_cos, row_sin = tables(NY)
    row_table = jnp.concatenate([row_cos, row_sin], 0).astype(jnp.bfloat16)
    col_cos, col_sin = tables(NZ)
    forward_block = jnp.block([[col_cos, -col_sin], [col_sin, col_cos]]).astype(jnp.bfloat16)
    adjoint_block = jnp.block([[col_cos, col_sin], [-col_sin, col_cos]]).astype(jnp.bfloat16)
    rounded = image.astype(jnp.bfloat16)
    sampled = sampling.astype(jnp.float32)[:, :, None, None, :]

    def per_coil(summed, coil_index):
        sensitivity = lax.dynamic_index_in_dim(coil_maps, coil_index, 1, keepdims=False).astype(jnp.float32)
        measured = lax.dynamic_index_in_dim(kspace, coil_index, 2, keepdims=False).astype(jnp.float32)
        weighted = complex_times(sensitivity[:, None], rounded.astype(jnp.float32), False).astype(jnp.bfloat16)
        halfway = column_section(weighted, forward_block).astype(jnp.bfloat16)
        spectrum = row_section(halfway, row_table, False)
        residual = (sampled * (spectrum - measured)).astype(jnp.bfloat16)
        backward = row_section(residual, row_table, True).astype(jnp.bfloat16)
        restored = column_section(backward, adjoint_block)
        return (summed + complex_times(sensitivity[:, None], restored, True), None)
    adjoint, _ = lax.scan(per_coil, jnp.zeros(image.shape, jnp.float32), jnp.arange(COILS, dtype=jnp.int32))
    padded = jnp.pad(rounded, ((1, 1), (0, 0), (1, 1), (0, 0), (1, 1))).astype(jnp.float32)
    lines, echoes, slices, parts, columns = image.shape

    def per_filter(summed, filter_pair):
        kernel, threshold = filter_pair
        kernel = kernel.astype(jnp.float32)
        response = jnp.zeros((lines, echoes, slices, columns), jnp.float32)
        for shift_y in range(3):
            for shift_r in range(3):
                for shift_z in range(3):
                    window = padded[shift_y:shift_y + lines, :, shift_r:shift_r + slices, :, shift_z:shift_z + columns]
                    response = response + kernel[shift_y, shift_r, shift_z, 0] * window[:, :, :, 0] + kernel[shift_y, shift_r, shift_z, 1] * window[:, :, :, 1]
        magnitude = jnp.sqrt(lax.optimization_barrier(jnp.sum(response * response, axis=1)))
        factor = magnitude / (magnitude + threshold)
        shrunk = (response * factor[:, None]).astype(jnp.bfloat16).astype(jnp.float32)
        shrunk_pad = jnp.pad(shrunk, ((1, 1), (0, 0), (1, 1), (1, 1)))
        contribution = jnp.zeros(image.shape, jnp.float32)
        for shift_y in range(3):
            for shift_r in range(3):
                for shift_z in range(3):
                    window = shrunk_pad[2 - shift_y:2 - shift_y + lines, :, 2 - shift_r:2 - shift_r + slices, 2 - shift_z:2 - shift_z + columns]
                    contribution = contribution + jnp.stack([kernel[shift_y, shift_r, shift_z, 0] * window, kernel[shift_y, shift_r, shift_z, 1] * window], -2)
        return (summed + contribution, None)
    penalty, _ = lax.scan(per_filter, jnp.zeros(image.shape, jnp.float32), (filters, thresholds))
    return image - dc_weight[None, :, None, None, None] * adjoint - penalty
```

```python
import functools

import numpy as np
import jax
import jax.numpy as jnp
from jax import lax
from jax.experimental import pallas as pl
from jax.experimental.pallas import tpu as pltpu
from jax.sharding import PartitionSpec as P

MESH = pl.DeviceIdType.MESH
F32 = jnp.float32
BF16 = jnp.bfloat16
SLAB = 32


def tables(length):
    product = np.outer(np.arange(length), np.arange(length)) % length
    phases = product * (2.0 * np.pi / length)
    normalize = length ** (-0.5)
    return np.cos(phases) * normalize, np.sin(phases) * normalize


def window_rows(rows, peers):
    for size in range(2, rows + 1):
        if rows % size == 0 and rows // size <= peers:
            return size
    return rows


def dot(left, right):
    return jnp.dot(left, right, preferred_element_type=F32)


def kernel(
    cfg,
    dc_ref, img_ref, xs_ref, kspace_hbm, maps_hbm, samp_hbm, fz_hbm, az_hbm, ty_hbm,
    wide_ref, tall_ref, thr_ref,
    adj_ref, pen_ref,
    gat, rs_send, rs_recv, ext, edge, pen_send, pen_recv, pacc, slab,
    kspace, maps, samp, fz, az, ty,
    local_sem, ag_send_sem, ag_recv_sem, x_send_sem, x_recv_sem, e_send_sem, e_recv_sem,
    p_send_sem, p_recv_sem, rs_send_sem, rs_recv_sem,
):
    n_e, n_c, n_r, n_q, rq, nz, ny = cfg
    peers = n_e * n_r
    e = lax.axis_index("echo")
    c = lax.axis_index("coil")
    r = lax.axis_index("read")
    q = e * n_r + r
    s_local, rb = rs_send.shape[0], img_ref.shape[0]
    width = 2 * nz
    zp = ext.shape[-1]

    loads = [
        pltpu.make_async_copy(src, dst, local_sem.at[i])
        for i, (src, dst) in enumerate(
            [(kspace_hbm, kspace), (maps_hbm, maps), (samp_hbm, samp), (fz_hbm, fz), (az_hbm, az), (ty_hbm, ty)]
        )
    ]

    def remote(src, dst, send, recv, target):
        return pltpu.make_async_remote_copy(
            src_ref=src, dst_ref=dst, send_sem=send, recv_sem=recv, device_id=target, device_id_type=MESH
        )

    def when(condition, act):
        if condition is True:
            act()
        else:
            pl.when(condition)(act)

    def up(d):
        return lax.rem(q + d, peers)

    def down(d):
        return lax.rem(q + peers - d, peers)

    def active(which):
        return True if n_q == peers else which < n_q

    barrier = pltpu.get_barrier_semaphore()
    for d in range(1, n_c):
        pl.semaphore_signal(barrier, inc=1, device_id=(e, lax.rem(c + d, n_c), r), device_id_type=MESH)
    for d in range(1, peers):
        pl.semaphore_signal(barrier, inc=1, device_id=(up(d) // n_r, c, lax.rem(up(d), n_r)), device_id_type=MESH)
        for step, ok in ((1, c < n_c - 1), (-1, c > 0)):
            @pl.when(ok)
            def _():
                pl.semaphore_signal(
                    barrier, inc=1, device_id=(up(d) // n_r, c + step, lax.rem(up(d), n_r)), device_id_type=MESH
                )
    sides = jnp.minimum(c, 1) + jnp.minimum(n_c - 1 - c, 1)
    pl.semaphore_wait(barrier, n_c - 1 + (peers - 1) * (1 + sides))

    def window(d):
        to = up(d)
        return remote(
            xs_ref.at[1 + to], ext.at[e, r], x_send_sem.at[d], x_recv_sem.at[d], (to // n_r, c, lax.rem(to, n_r))
        )

    last = n_q - 1
    edge_up = lambda: remote(
        xs_ref.at[n_q + 1], edge.at[e, r], e_send_sem.at[0], e_recv_sem.at[q], (0, c + 1, 0)
    )
    edge_down = lambda: remote(
        xs_ref.at[0], edge.at[e, r], e_send_sem.at[1], e_recv_sem.at[q], (last // n_r, c - 1, last % n_r)
    )
    for d in range(1, peers):
        when(active(up(d)), lambda: window(d).start())
    pl.when(c < n_c - 1)(lambda: edge_up().start())
    pl.when(c > 0)(lambda: edge_down().start())

    def gather(d):
        return remote(
            img_ref, gat.at[c], ag_send_sem.at[d], ag_recv_sem.at[d], (e, lax.rem(c + d, n_c), r)
        )

    for d in range(1, n_c):
        gather(d).start()
    for load in loads:
        load.start()
    gat[c] = img_ref[...]

    has_edge = jnp.logical_or(
        jnp.logical_and(q == 0, c > 0), jnp.logical_and(q == last, c < n_c - 1)
    )

    @pl.when(jnp.logical_not(has_edge))
    def _():
        edge[...] = jnp.zeros_like(edge)

    def regularize():
        ext[e, r] = xs_ref[1 + q]
        for d in range(1, peers):
            src = down(d)
            remote(
                xs_ref.at[0], ext.at[src // n_r, lax.rem(src, n_r)], x_send_sem.at[d], x_recv_sem.at[d], (e, c, r)
            ).wait_recv()

        @pl.when(has_edge)
        def _():
            for src in range(peers):
                remote(
                    xs_ref.at[0], edge.at[src // n_r, src % n_r], e_send_sem.at[0], e_recv_sem.at[src], (e, c, r)
                ).wait_recv()

        rows = rq + 4
        taps = 2 * s_local * n_r
        for echo in range(n_e):
            parts = [ext[echo, read].astype(F32) + edge[echo, read].astype(F32) for read in range(n_r)]
            block = jnp.concatenate(parts, axis=1) if n_r > 1 else parts[0]
            flat = block.reshape(rows * taps, zp)
            moved = [
                pltpu.roll(flat, 1, 1).reshape(rows, taps, zp),
                block,
                pltpu.roll(flat, zp - 1, 1).reshape(rows, taps, zp),
            ]
            fill = [jnp.zeros((rows, SLAB - 3 * taps, zp), F32)] if SLAB > 3 * taps else []
            slab[echo] = jnp.concatenate(moved + fill, axis=1).reshape(rows * SLAB, zp).astype(BF16)

        pacc[...] = jnp.zeros_like(pacc)
        tall = tall_ref[...]
        wide = wide_ref[...]
        lane_ok = lax.broadcasted_iota(jnp.int32, (1, zp), 1) < nz
        first = c * rb + q * rq - 1

        def row(i, carry):
            start = pl.multiple_of(i * SLAB, SLAB)
            response = [dot(tall, slab[echo, pl.ds(start, 3 * SLAB), :]) for echo in range(n_e)]
            energy = response[0] * response[0]
            for other in response[1:]:
                energy = energy + other * other
            magnitude = jnp.sqrt(energy)
            factor = magnitude / (magnitude + thr_ref[...])
            inside = jnp.logical_and(first + i >= 0, first + i < ny)
            factor = jnp.where(jnp.logical_and(lane_ok, inside), factor, 0.0)
            for echo in range(n_e):
                spread = dot(wide, (response[echo] * factor).astype(BF16))
                for a in range(3):
                    pacc[echo, i + a] += spread[a * SLAB : (a + 1) * SLAB]
            return carry

        lax.fori_loop(0, rq + 2, row, 0, unroll=2)
        for echo in range(n_e):
            held = pacc[echo, 2 : 2 + rq]
            low = pltpu.roll(held[:, :taps].reshape(rq * taps, zp), zp - 1, 1).reshape(rq, taps, zp)
            high = pltpu.roll(held[:, 2 * taps : 3 * taps].reshape(rq * taps, zp), 1, 1).reshape(rq, taps, zp)
            total = low + held[:, taps : 2 * taps] + high
            for read in range(n_r):
                pen_send[echo, read] = total[:, read * 2 * s_local : (read + 1) * 2 * s_local]
        pen_recv[q] = pen_send[e, r]

    def penalty_out(d):
        to = up(d)
        return remote(
            pen_send.at[to // n_r, lax.rem(to, n_r)], pen_recv.at[q], p_send_sem.at[d], p_recv_sem.at[d],
            (to // n_r, c, lax.rem(to, n_r)),
        )

    def all_penalties():
        regularize()
        for d in range(1, peers):
            penalty_out(d).start()

    when(active(q), all_penalties)

    for d in range(1, n_c):
        src = lax.rem(c + n_c - d, n_c)
        remote(img_ref, gat.at[src], ag_send_sem.at[d], ag_recv_sem.at[d], (e, c, r)).wait_recv()
    for load in loads:
        load.wait()

    def scatter(s, d):
        to = lax.rem(c + d, n_c)
        return remote(
            rs_send.at[s, to], rs_recv.at[s, c], rs_send_sem.at[s, d], rs_recv_sem.at[s, d], (e, to, r)
        )

    sampled = samp[...].astype(F32)
    for s in range(s_local):
        image = gat[:, :, s * width : (s + 1) * width].astype(F32).reshape(ny, width).T
        real, imag = image[:nz], image[nz:]
        map_real, map_imag = maps[s, 0].astype(F32), maps[s, 1].astype(F32)
        weighted = jnp.concatenate(
            [map_real * real - map_imag * imag, map_real * imag + map_imag * real], 0
        ).astype(BF16)
        halfway = dot(fz[...], weighted).astype(BF16)
        spectrum = dot(halfway, ty[...])
        spec_real = spectrum[:nz, :ny] + spectrum[nz:, ny:]
        spec_imag = spectrum[nz:, :ny] - spectrum[:nz, ny:]
        residual = jnp.concatenate(
            [
                sampled * (spec_real - kspace[s, 0].astype(F32)),
                sampled * (spec_imag - kspace[s, 1].astype(F32)),
            ],
            0,
        ).astype(BF16)
        returned = dot(residual, ty[...])
        backward = jnp.concatenate(
            [returned[:nz, :ny] - returned[nz:, ny:], returned[nz:, :ny] + returned[:nz, ny:]], 0
        ).astype(BF16)
        restored = dot(az[...], backward)
        back_real, back_imag = restored[:nz], restored[nz:]
        map_real, map_imag = maps[s, 0].astype(F32), maps[s, 1].astype(F32)
        adjoint = jnp.concatenate(
            [map_real * back_real + map_imag * back_imag, map_real * back_imag - map_imag * back_real], 0
        ).T
        rs_send[s] = adjoint.reshape(n_c, rb, width).astype(BF16)
        for d in range(1, n_c):
            scatter(s, d).start()

    for d in range(1, peers):
        src = down(d)
        when(
            active(src),
            lambda: remote(
                pen_send.at[0, 0], pen_recv.at[src], p_send_sem.at[d], p_recv_sem.at[d], (e, c, r)
            ).wait_recv(),
        )
    pen_ref[...] = pen_recv[...].reshape(rb, 2 * s_local, zp)

    dc = dc_ref[0]
    for s in range(s_local):
        total = rs_send[s, c].astype(F32)
        for d in range(1, n_c):
            src = lax.rem(c + n_c - d, n_c)
            remote(
                rs_send.at[s, src], rs_recv.at[s, src], rs_send_sem.at[s, d], rs_recv_sem.at[s, d], (e, c, r)
            ).wait_recv()
            total = total + rs_recv[s, src].astype(F32)
        adj_ref[:, s * width : (s + 1) * width] = dc * total

    for d in range(1, n_c):
        gather(d).wait_send()
        for s in range(s_local):
            scatter(s, d).wait_send()
    for d in range(1, peers):
        when(active(up(d)), lambda: window(d).wait_send())
        when(active(q), lambda: penalty_out(d).wait_send())
    pl.when(c < n_c - 1)(lambda: edge_up().wait_send())
    pl.when(c > 0)(lambda: edge_down().wait_send())


def body(kspace, sampling, coil_maps, image, filters, thresholds, dc_weight):
    n_e, n_c, n_r = lax.axis_size("echo"), lax.axis_size("coil"), lax.axis_size("read")
    rb, _, s_local, _, nz = image.shape
    ny = kspace.shape[0]
    peers = n_e * n_r
    rq = window_rows(rb, peers)
    n_q = rb // rq
    zp = -(-(nz + 1) // 128) * 128
    width = 2 * nz
    slices = s_local * n_r
    taps = 2 * slices
    count = filters.shape[0]

    col_cos, col_sin = tables(nz)
    row_cos, row_sin = tables(ny)
    fz = jnp.asarray(np.block([[col_cos, col_sin], [-col_sin, col_cos]]), BF16)
    az = jnp.asarray(np.block([[col_cos, -col_sin], [col_sin, col_cos]]), BF16)
    ty = jnp.asarray(np.concatenate([row_cos, row_sin], 1), BF16)

    rounded = image.astype(BF16)
    flat = rounded.reshape(rb, s_local * width)
    rows = rounded.reshape(rb, 2 * s_local, nz)
    margin = rq + 2
    padded = jnp.pad(rows, ((margin, margin), (0, 0), (0, zp - nz)))
    xs = jnp.stack([padded[j * rq : j * rq + rq + 4] for j in range(n_q + 2)])

    taps_of = jnp.transpose(filters, (1, 3, 2, 4, 0))
    shifted = jnp.stack(
        [
            jnp.pad(taps_of, ((0, 0), (0, 0), (at, slices - 1 - at), (0, 0), (0, 0)))[:, :, 1 : slices + 1]
            for at in range(slices)
        ],
        4,
    )
    wide = jnp.pad(
        shifted.reshape(3, 3 * taps, slices * count), ((0, 0), (0, SLAB - 3 * taps), (0, 0))
    ).reshape(3 * SLAB, slices * count)
    tall = wide.T
    thr = jnp.tile(thresholds, slices)[:, None]

    k_view = jnp.transpose(kspace[:, 0, 0], (1, 2, 3, 0))
    m_view = jnp.transpose(coil_maps[:, 0], (1, 2, 3, 0))
    s_view = jnp.transpose(sampling[:, 0], (1, 0))

    vmem = pl.BlockSpec(memory_space=pltpu.VMEM)
    hbm = pl.BlockSpec(memory_space=pl.ANY)
    smem = pl.BlockSpec(memory_space=pltpu.SMEM)
    dma = pltpu.SemaphoreType.DMA
    total, penalty = pl.pallas_call(
        functools.partial(kernel, (n_e, n_c, n_r, n_q, rq, nz, ny)),
        out_shape=(
            jax.ShapeDtypeStruct((rb, s_local * width), F32),
            jax.ShapeDtypeStruct((rb, 2 * s_local, zp), F32),
        ),
        in_specs=[smem, vmem, vmem, hbm, hbm, hbm, hbm, hbm, hbm, vmem, vmem, vmem],
        out_specs=(vmem, vmem),
        scratch_shapes=[
            pltpu.VMEM((n_c, rb, s_local * width), BF16),
            pltpu.VMEM((s_local, n_c, rb, width), BF16),
            pltpu.VMEM((s_local, n_c, rb, width), BF16),
            pltpu.VMEM((n_e, n_r, rq + 4, 2 * s_local, zp), BF16),
            pltpu.VMEM((n_e, n_r, rq + 4, 2 * s_local, zp), BF16),
            pltpu.VMEM((n_e, n_r, rq, 2 * s_local, zp), F32),
            pltpu.VMEM((n_q, rq, 2 * s_local, zp), F32),
            pltpu.VMEM((n_e, rq + 4, SLAB, zp), F32),
            pltpu.VMEM((n_e, (rq + 4) * SLAB, zp), BF16),
            pltpu.VMEM(k_view.shape, BF16),
            pltpu.VMEM(m_view.shape, BF16),
            pltpu.VMEM(s_view.shape, jnp.int32),
            pltpu.VMEM(fz.shape, BF16),
            pltpu.VMEM(az.shape, BF16),
            pltpu.VMEM(ty.shape, BF16),
            dma((6,)),
            dma((n_c,)), dma((n_c,)),
            dma((peers,)), dma((peers,)),
            dma((2,)), dma((peers,)),
            dma((peers,)), dma((peers,)),
            dma((s_local, n_c)), dma((s_local, n_c)),
        ],
        compiler_params=pltpu.CompilerParams(
            collective_id=0, has_side_effects=True, vmem_limit_bytes=56 << 20
        ),
        name="cascade",
    )(dc_weight, flat, xs, k_view, m_view, s_view, fz, az, ty, wide, tall, thr)
    shape = image.shape
    return image - total.reshape(shape) - penalty[:, :, :nz].reshape(shape)


def solution(mesh):
    return jax.shard_map(
        body,
        mesh=mesh,
        in_specs=(
            P(None, "echo", "coil", "read", None, None),
            P(None, "echo", None),
            P(None, "coil", "read", None, None),
            P("coil", "echo", "read", None, None),
            P(),
            P(),
            P("echo"),
        ),
        out_specs=P("coil", "echo", "read", None, None),
        check_vma=False,
    )
```

```python
import functools

import numpy as np
import jax
import jax.numpy as jnp
from jax import lax
from jax.experimental import pallas as pl
from jax.experimental.pallas import tpu as pltpu
from jax.sharding import PartitionSpec as P

MESH = pl.DeviceIdType.MESH
F32 = jnp.float32
BF16 = jnp.bfloat16
SLAB = 32


def tables(length):
    product = np.outer(np.arange(length), np.arange(length)) % length
    phases = product * (2.0 * np.pi / length)
    normalize = length ** (-0.5)
    return np.cos(phases) * normalize, np.sin(phases) * normalize


def window_rows(rows, peers):
    for size in range(2, rows + 1):
        if rows % size == 0 and rows // size <= peers:
            return size
    return rows


def dot(left, right):
    return jnp.dot(left, right, preferred_element_type=F32)


def kernel(
    cfg,
    dc_ref, img_ref, xs_ref, kspace_hbm, maps_hbm, samp_hbm, fz_hbm, az_hbm, ty_hbm,
    filters_ref, spread_ref, thr_ref,
    adj_ref, pen_ref,
    gat, part, paired, rs_send, rs_recv, wide_ref, tall_ref, level, ext, edge, pen_send, pen_recv, pacc, slab,
    kspace, maps, samp, fz, az, ty,
    local_sem, ag_send_sem, ag_recv_sem, x_send_sem, x_recv_sem, e_send_sem, e_recv_sem,
    p_send_sem, p_recv_sem, rs_send_sem, rs_recv_sem, f_send_sem, f_recv_sem, pair_send_sem, pair_recv_sem,
):
    n_e, n_c, n_r, n_q, rq, nz, ny = cfg
    peers = n_e * n_r
    e = lax.axis_index("echo")
    c = lax.axis_index("coil")
    r = lax.axis_index("read")
    q = e * n_r + r
    s_local, rb = rs_send.shape[0], img_ref.shape[0]
    chips = n_c // 2
    core = lax.rem(c, 2)
    chip = c // 2
    partner = c + 1 - 2 * core
    width = 2 * nz
    zp = ext.shape[-1]

    loads = [
        pltpu.make_async_copy(src, dst, local_sem.at[i])
        for i, (src, dst) in enumerate(
            [(kspace_hbm, kspace), (maps_hbm, maps), (samp_hbm, samp), (fz_hbm, fz), (az_hbm, az), (ty_hbm, ty)]
        )
    ]

    def remote(src, dst, send, recv, target):
        return pltpu.make_async_remote_copy(
            src_ref=src, dst_ref=dst, send_sem=send, recv_sem=recv, device_id=target, device_id_type=MESH
        )

    def when(condition, act):
        if condition is True:
            act()
        else:
            pl.when(condition)(act)

    def up(d):
        return lax.rem(q + d, peers)

    def down(d):
        return lax.rem(q + peers - d, peers)

    def active(which):
        return True if n_q == peers else which < n_q

    barrier = pltpu.get_barrier_semaphore()
    for d in range(chips):
        to = lax.rem(c + 2 * d, n_c) if d else partner
        pl.semaphore_signal(barrier, inc=1, device_id=(e, to, r), device_id_type=MESH)
    for d in range(peers):
        if d:
            pl.semaphore_signal(barrier, inc=1, device_id=(up(d) // n_r, c, lax.rem(up(d), n_r)), device_id_type=MESH)
        for step, ok in ((1, c < n_c - 1), (-1, c > 0)):
            @pl.when(ok)
            def _():
                pl.semaphore_signal(
                    barrier, inc=1, device_id=(up(d) // n_r, c + step, lax.rem(up(d), n_r)), device_id_type=MESH
                )
    sides = jnp.minimum(c, 1) + jnp.minimum(n_c - 1 - c, 1)
    pl.semaphore_wait(barrier, chips + peers - 1 + peers * sides)

    def window(d):
        to = up(d)
        return remote(
            xs_ref.at[1 + to], ext.at[e, r], x_send_sem.at[d], x_recv_sem.at[d], (to // n_r, c, lax.rem(to, n_r))
        )

    last = n_q - 1
    edge_up = lambda: remote(
        xs_ref.at[n_q + 1], edge.at[e, r], e_send_sem.at[0], e_recv_sem.at[q], (0, c + 1, 0)
    )
    edge_down = lambda: remote(
        xs_ref.at[0], edge.at[e, r], e_send_sem.at[1], e_recv_sem.at[q], (last // n_r, c - 1, last % n_r)
    )
    for d in range(1, peers):
        when(active(up(d)), lambda: window(d).start())
    pl.when(c < n_c - 1)(lambda: edge_up().start())
    pl.when(c > 0)(lambda: edge_down().start())

    def gather(d):
        to = lax.rem(c + 2 * d, n_c) if d else partner
        return remote(img_ref, gat.at[c], ag_send_sem.at[d], ag_recv_sem.at[d], (e, to, r))

    def forward(d):
        src = lax.rem(c + n_c - 2 * d, n_c)
        return remote(gat.at[src], gat.at[src], f_send_sem.at[d], f_recv_sem.at[d], (e, partner, r))

    for d in range(chips):
        gather(d).start()
    for load in loads:
        load.start()
    gat[c] = img_ref[...]

    count = filters_ref.shape[-1]
    slices = s_local * n_r
    flat_filters = filters_ref[...]
    pieces = [dot(spread_ref[at], flat_filters) for at in range(slices)]
    for at in range(slices):
        wide_ref[:, at * count : (at + 1) * count] = pieces[at].astype(BF16)
        tall_ref[at * count : (at + 1) * count, :] = pieces[at].T.astype(BF16)
    shape = (slices, count, count)
    on = lax.broadcasted_iota(jnp.int32, shape, 1) == lax.broadcasted_iota(jnp.int32, shape, 2)
    column = jnp.sum(jnp.where(on, thr_ref[...].reshape(1, 1, count), 0.0), axis=2, keepdims=True)
    level[...] = jnp.broadcast_to(column, (slices, count, zp)).reshape(slices * count, zp)

    has_edge = jnp.logical_or(
        jnp.logical_and(q == 0, c > 0), jnp.logical_and(q == last, c < n_c - 1)
    )

    @pl.when(jnp.logical_not(has_edge))
    def _():
        edge[...] = jnp.zeros_like(edge)

    def regularize():
        ext[e, r] = xs_ref[1 + q]
        for d in range(1, peers):
            src = down(d)
            remote(
                xs_ref.at[0], ext.at[src // n_r, lax.rem(src, n_r)], x_send_sem.at[d], x_recv_sem.at[d], (e, c, r)
            ).wait_recv()

        @pl.when(has_edge)
        def _():
            for src in range(peers):
                remote(
                    xs_ref.at[0], edge.at[src // n_r, src % n_r], e_send_sem.at[0], e_recv_sem.at[src], (e, c, r)
                ).wait_recv()

        rows = rq + 4
        taps = 2 * s_local * n_r
        for echo in range(n_e):
            parts = [ext[echo, read].astype(F32) + edge[echo, read].astype(F32) for read in range(n_r)]
            block = jnp.concatenate(parts, axis=1) if n_r > 1 else parts[0]
            flat = block.reshape(rows * taps, zp)
            moved = [
                pltpu.roll(flat, 1, 1).reshape(rows, taps, zp),
                block,
                pltpu.roll(flat, zp - 1, 1).reshape(rows, taps, zp),
            ]
            fill = [jnp.zeros((rows, SLAB - 3 * taps, zp), F32)] if SLAB > 3 * taps else []
            slab[echo] = jnp.concatenate(moved + fill, axis=1).reshape(rows * SLAB, zp).astype(BF16)

        pacc[...] = jnp.zeros_like(pacc)
        tall = tall_ref[...]
        wide = wide_ref[...]
        lane_ok = lax.broadcasted_iota(jnp.int32, (1, zp), 1) < nz
        first = c * rb + q * rq - 1

        def row(i, carry):
            start = pl.multiple_of(i * SLAB, SLAB)
            response = [dot(tall, slab[echo, pl.ds(start, 3 * SLAB), :]) for echo in range(n_e)]
            energy = response[0] * response[0]
            for other in response[1:]:
                energy = energy + other * other
            magnitude = jnp.sqrt(energy)
            factor = magnitude / (magnitude + level[...])
            inside = jnp.logical_and(first + i >= 0, first + i < ny)
            factor = jnp.where(jnp.logical_and(lane_ok, inside), factor, 0.0)
            for echo in range(n_e):
                spread = dot(wide, (response[echo] * factor).astype(BF16))
                for a in range(3):
                    pacc[echo, i + a] += spread[a * SLAB : (a + 1) * SLAB]
            return carry

        lax.fori_loop(0, rq + 2, row, 0, unroll=2)
        for echo in range(n_e):
            held = pacc[echo, 2 : 2 + rq]
            low = pltpu.roll(held[:, :taps].reshape(rq * taps, zp), zp - 1, 1).reshape(rq, taps, zp)
            high = pltpu.roll(held[:, 2 * taps : 3 * taps].reshape(rq * taps, zp), 1, 1).reshape(rq, taps, zp)
            total = low + held[:, taps : 2 * taps] + high
            for read in range(n_r):
                pen_send[echo, read] = total[:, read * 2 * s_local : (read + 1) * 2 * s_local]
        pen_recv[q] = pen_send[e, r]

    def penalty_out(d):
        to = up(d)
        return remote(
            pen_send.at[to // n_r, lax.rem(to, n_r)], pen_recv.at[q], p_send_sem.at[d], p_recv_sem.at[d],
            (to // n_r, c, lax.rem(to, n_r)),
        )

    def all_penalties():
        regularize()
        for d in range(1, peers):
            penalty_out(d).start()

    when(active(q), all_penalties)

    for d in range(1, chips):
        src = lax.rem(c + n_c - 2 * d, n_c)
        remote(img_ref, gat.at[src], ag_send_sem.at[d], ag_recv_sem.at[d], (e, partner, r)).wait_recv()
        forward(d).start()
    remote(img_ref, gat.at[partner], ag_send_sem.at[0], ag_recv_sem.at[0], (e, partner, r)).wait_recv()
    for d in range(1, chips):
        src = lax.rem(partner + n_c - 2 * d, n_c)
        remote(gat.at[src], gat.at[src], f_send_sem.at[d], f_recv_sem.at[d], (e, partner, r)).wait_recv()
    for load in loads:
        load.wait()

    def pair(s):
        return remote(
            part.at[s, :, 1 - core], paired.at[s], pair_send_sem.at[s], pair_recv_sem.at[s], (e, partner, r)
        )

    def scatter(s, d):
        to = lax.rem(chip + d, chips)
        return remote(
            rs_send.at[s, to], rs_recv.at[s, chip], rs_send_sem.at[s, d], rs_recv_sem.at[s, d],
            (e, 2 * to + core, r),
        )

    def send_sums(s):
        pair(s).wait_recv()
        rs_send[s] = (part[s, :, core].astype(F32) + paired[s].astype(F32)).astype(BF16)
        for d in range(1, chips):
            scatter(s, d).start()

    sampled = samp[...].astype(F32)
    for s in range(s_local):
        image = gat[:, :, s * width : (s + 1) * width].astype(F32).reshape(ny, width).T
        real, imag = image[:nz], image[nz:]
        map_real, map_imag = maps[s, 0].astype(F32), maps[s, 1].astype(F32)
        weighted = jnp.concatenate(
            [map_real * real - map_imag * imag, map_real * imag + map_imag * real], 0
        ).astype(BF16)
        halfway = dot(fz[...], weighted).astype(BF16)
        spectrum = dot(halfway, ty[...])
        if s:
            send_sums(s - 1)
        spec_real = spectrum[:nz, :ny] + spectrum[nz:, ny:]
        spec_imag = spectrum[nz:, :ny] - spectrum[:nz, ny:]
        residual = jnp.concatenate(
            [
                sampled * (spec_real - kspace[s, 0].astype(F32)),
                sampled * (spec_imag - kspace[s, 1].astype(F32)),
            ],
            0,
        ).astype(BF16)
        returned = dot(residual, ty[...])
        backward = jnp.concatenate(
            [returned[:nz, :ny] - returned[nz:, ny:], returned[nz:, :ny] + returned[:nz, ny:]], 0
        ).astype(BF16)
        restored = dot(az[...], backward)
        back_real, back_imag = restored[:nz], restored[nz:]
        map_real, map_imag = maps[s, 0].astype(F32), maps[s, 1].astype(F32)
        adjoint = jnp.concatenate(
            [map_real * back_real + map_imag * back_imag, map_real * back_imag - map_imag * back_real], 0
        ).T
        part[s] = adjoint.reshape(chips, 2, rb, width).astype(BF16)
        pair(s).start()
    send_sums(s_local - 1)

    for d in range(1, peers):
        src = down(d)
        when(
            active(src),
            lambda: remote(
                pen_send.at[0, 0], pen_recv.at[src], p_send_sem.at[d], p_recv_sem.at[d], (e, c, r)
            ).wait_recv(),
        )
    pen_ref[...] = pen_recv[...].reshape(rb, 2 * s_local, zp)

    dc = dc_ref[0]
    for s in range(s_local):
        total = part[s, chip, core].astype(F32) + paired[s, chip].astype(F32)
        for d in range(1, chips):
            src = lax.rem(chip + chips - d, chips)
            remote(
                rs_send.at[s, src], rs_recv.at[s, src], rs_send_sem.at[s, d], rs_recv_sem.at[s, d], (e, partner, r)
            ).wait_recv()
            total = total + rs_recv[s, src].astype(F32)
        adj_ref[:, s * width : (s + 1) * width] = dc * total

    for d in range(chips):
        gather(d).wait_send()
        if d:
            forward(d).wait_send()
            for s in range(s_local):
                scatter(s, d).wait_send()
    for s in range(s_local):
        pair(s).wait_send()
    for d in range(1, peers):
        when(active(up(d)), lambda: window(d).wait_send())
        when(active(q), lambda: penalty_out(d).wait_send())
    pl.when(c < n_c - 1)(lambda: edge_up().wait_send())
    pl.when(c > 0)(lambda: edge_down().wait_send())


def body(kspace, sampling, coil_maps, image, filters, thresholds, dc_weight):
    n_e, n_c, n_r = lax.axis_size("echo"), lax.axis_size("coil"), lax.axis_size("read")
    rb, _, s_local, _, nz = image.shape
    ny = kspace.shape[0]
    peers = n_e * n_r
    rq = window_rows(rb, peers)
    n_q = rb // rq
    zp = -(-(nz + 1) // 128) * 128
    width = 2 * nz
    slices = s_local * n_r
    taps = 2 * slices
    count = filters.shape[0]

    col_cos, col_sin = tables(nz)
    row_cos, row_sin = tables(ny)
    fz = jnp.asarray(np.block([[col_cos, col_sin], [-col_sin, col_cos]]), BF16)
    az = jnp.asarray(np.block([[col_cos, -col_sin], [col_sin, col_cos]]), BF16)
    ty = jnp.asarray(np.concatenate([row_cos, row_sin], 1), BF16)

    rounded = image.astype(BF16)
    flat = rounded.reshape(rb, s_local * width)
    rows = rounded.reshape(rb, 2 * s_local, nz)
    margin = rq + 2
    padded = jnp.pad(rows, ((margin, margin), (0, 0), (0, zp - nz)))
    xs = jnp.stack([padded[j * rq : j * rq + rq + 4] for j in range(n_q + 2)])

    spread = np.zeros((slices, 3, SLAB, 3, 3, 3, 2))
    for at in range(slices):
        for a in range(3):
            for b in range(3):
                for d in range(3):
                    for p in range(2):
                        if 0 <= at + b - 1 < slices:
                            spread[at, a, d * taps + (at + b - 1) * 2 + p, a, b, d, p] = 1.0
    spread = jnp.asarray(spread.reshape(slices, 3 * SLAB, 54), BF16)
    flat_filters = filters.reshape(count, 54).T
    thr = thresholds[None, :]

    k_view = jnp.transpose(kspace[:, 0, 0], (1, 2, 3, 0))
    m_view = jnp.transpose(coil_maps[:, 0], (1, 2, 3, 0))
    s_view = jnp.transpose(sampling[:, 0], (1, 0))

    vmem = pl.BlockSpec(memory_space=pltpu.VMEM)
    hbm = pl.BlockSpec(memory_space=pl.ANY)
    smem = pl.BlockSpec(memory_space=pltpu.SMEM)
    dma = pltpu.SemaphoreType.DMA
    total, penalty = pl.pallas_call(
        functools.partial(kernel, (n_e, n_c, n_r, n_q, rq, nz, ny)),
        out_shape=(
            jax.ShapeDtypeStruct((rb, s_local * width), F32),
            jax.ShapeDtypeStruct((rb, 2 * s_local, zp), F32),
        ),
        in_specs=[smem, vmem, vmem, hbm, hbm, hbm, hbm, hbm, hbm, vmem, vmem, vmem],
        out_specs=(vmem, vmem),
        scratch_shapes=[
            pltpu.VMEM((n_c, rb, s_local * width), BF16),
            pltpu.VMEM((s_local, n_c // 2, 2, rb, width), BF16),
            pltpu.VMEM((s_local, n_c // 2, rb, width), BF16),
            pltpu.VMEM((s_local, n_c // 2, rb, width), BF16),
            pltpu.VMEM((s_local, n_c // 2, rb, width), BF16),
            pltpu.VMEM((3 * SLAB, slices * count), BF16),
            pltpu.VMEM((slices * count, 3 * SLAB), BF16),
            pltpu.VMEM((slices * count, zp), F32),
            pltpu.VMEM((n_e, n_r, rq + 4, 2 * s_local, zp), BF16),
            pltpu.VMEM((n_e, n_r, rq + 4, 2 * s_local, zp), BF16),
            pltpu.VMEM((n_e, n_r, rq, 2 * s_local, zp), F32),
            pltpu.VMEM((n_q, rq, 2 * s_local, zp), F32),
            pltpu.VMEM((n_e, rq + 4, SLAB, zp), F32),
            pltpu.VMEM((n_e, (rq + 4) * SLAB, zp), BF16),
            pltpu.VMEM(k_view.shape, BF16),
            pltpu.VMEM(m_view.shape, BF16),
            pltpu.VMEM(s_view.shape, jnp.int32),
            pltpu.VMEM(fz.shape, BF16),
            pltpu.VMEM(az.shape, BF16),
            pltpu.VMEM(ty.shape, BF16),
            dma((6,)),
            dma((n_c,)), dma((n_c,)),
            dma((peers,)), dma((peers,)),
            dma((2,)), dma((peers,)),
            dma((peers,)), dma((peers,)),
            dma((s_local, n_c)), dma((s_local, n_c)),
            dma((n_c,)), dma((n_c,)), dma((s_local,)), dma((s_local,)),
        ],
        compiler_params=pltpu.CompilerParams(
            collective_id=0, has_side_effects=True, vmem_limit_bytes=56 << 20
        ),
        name="cascade",
    )(dc_weight, flat, xs, k_view, m_view, s_view, fz, az, ty, flat_filters, spread, thr)
    shape = image.shape
    return image - total.reshape(shape) - penalty[:, :, :nz].reshape(shape)


def solution(mesh):
    return jax.shard_map(
        body,
        mesh=mesh,
        in_specs=(
            P(None, "echo", "coil", "read", None, None),
            P(None, "echo", None),
            P(None, "coil", "read", None, None),
            P("coil", "echo", "read", None, None),
            P(),
            P(),
            P("echo"),
        ),
        out_specs=P("coil", "echo", "read", None, None),
        check_vma=False,
    )
```

```python
import functools

import numpy as np
import jax
import jax.numpy as jnp
from jax import lax
from jax.experimental import pallas as pl
from jax.experimental.pallas import tpu as pltpu
from jax.sharding import PartitionSpec as P

MESH = pl.DeviceIdType.MESH
F32 = jnp.float32
BF16 = jnp.bfloat16
SLAB = 32
GRANT = 24 << 20


def tables(length):
    product = np.outer(np.arange(length), np.arange(length)) % length
    phases = product * (2.0 * np.pi / length)
    normalize = length ** (-0.5)
    return np.cos(phases) * normalize, np.sin(phases) * normalize


def window_rows(rows, peers):
    for size in range(2, rows + 1):
        if rows % size == 0 and rows // size <= peers:
            return size
    return rows


def dot(left, right):
    return jnp.dot(left, right, preferred_element_type=F32)


def kernel(
    cfg,
    dc_ref, img_ref, xs_ref, kspace_hbm, maps_hbm, samp_hbm, fz_hbm, az_hbm, ty_hbm,
    filters_ref, spread_ref, thr_ref,
    adj_ref, pen_ref,
    gat, part, paired, rs_send, rs_recv, wide_ref, tall_ref, level, ext, edge, pen_send, pen_recv, pacc, slab,
    kspace, maps, samp, fz, az, ty,
    local_sem, ag_send_sem, ag_recv_sem, x_send_sem, x_recv_sem, e_send_sem, e_recv_sem,
    p_send_sem, p_recv_sem, rs_send_sem, rs_recv_sem, f_send_sem, f_recv_sem, pair_send_sem, pair_recv_sem,
):
    n_e, n_c, n_r, n_q, rq, nz, ny = cfg
    peers = n_e * n_r
    e = lax.axis_index("echo")
    c = lax.axis_index("coil")
    r = lax.axis_index("read")
    q = e * n_r + r
    s_local, rb = rs_send.shape[0], img_ref.shape[0]
    chips = n_c // 2
    core = lax.rem(c, 2)
    chip = c // 2
    partner = c + 1 - 2 * core
    width = 2 * nz
    zp = ext.shape[-1]

    loads = [
        pltpu.make_async_copy(src, dst, local_sem.at[i])
        for i, (src, dst) in enumerate(
            [(kspace_hbm, kspace), (maps_hbm, maps), (samp_hbm, samp), (fz_hbm, fz), (az_hbm, az), (ty_hbm, ty)]
        )
    ]

    def remote(src, dst, send, recv, target):
        return pltpu.make_async_remote_copy(
            src_ref=src, dst_ref=dst, send_sem=send, recv_sem=recv, device_id=target, device_id_type=MESH
        )

    def when(condition, act):
        if condition is True:
            act()
        else:
            pl.when(condition)(act)

    def up(d):
        return lax.rem(q + d, peers)

    def down(d):
        return lax.rem(q + peers - d, peers)

    def active(which):
        return True if n_q == peers else which < n_q

    barrier = pltpu.get_barrier_semaphore()
    for d in range(chips):
        to = lax.rem(c + 2 * d, n_c) if d else partner
        pl.semaphore_signal(barrier, inc=1, device_id=(e, to, r), device_id_type=MESH)
    for d in range(peers):
        if d:
            pl.semaphore_signal(barrier, inc=1, device_id=(up(d) // n_r, c, lax.rem(up(d), n_r)), device_id_type=MESH)
        for step, ok in ((1, c < n_c - 1), (-1, c > 0)):
            @pl.when(ok)
            def _():
                pl.semaphore_signal(
                    barrier, inc=1, device_id=(up(d) // n_r, c + step, lax.rem(up(d), n_r)), device_id_type=MESH
                )
    sides = jnp.minimum(c, 1) + jnp.minimum(n_c - 1 - c, 1)
    pl.semaphore_wait(barrier, chips + peers - 1 + peers * sides)

    def window(d):
        to = up(d)
        return remote(
            xs_ref.at[1 + to], ext.at[e, r], x_send_sem.at[d], x_recv_sem.at[d], (to // n_r, c, lax.rem(to, n_r))
        )

    last = n_q - 1
    edge_up = lambda: remote(
        xs_ref.at[n_q + 1], edge.at[e, r], e_send_sem.at[0], e_recv_sem.at[q], (0, c + 1, 0)
    )
    edge_down = lambda: remote(
        xs_ref.at[0], edge.at[e, r], e_send_sem.at[1], e_recv_sem.at[q], (last // n_r, c - 1, last % n_r)
    )
    for d in range(1, peers):
        when(active(up(d)), lambda: window(d).start())
    pl.when(c < n_c - 1)(lambda: edge_up().start())
    pl.when(c > 0)(lambda: edge_down().start())

    def gather(d):
        to = lax.rem(c + 2 * d, n_c) if d else partner
        return remote(img_ref, gat.at[c], ag_send_sem.at[d], ag_recv_sem.at[d], (e, to, r))

    def forward(d):
        src = lax.rem(c + n_c - 2 * d, n_c)
        return remote(gat.at[src], gat.at[src], f_send_sem.at[d], f_recv_sem.at[d], (e, partner, r))

    for d in range(chips):
        gather(d).start()
    for load in loads:
        load.start()
    gat[c] = img_ref[...]

    count = filters_ref.shape[-1]
    slices = s_local * n_r
    flat_filters = filters_ref[...].astype(F32).reshape(-1, count).astype(BF16)
    pieces = [dot(spread_ref[at], flat_filters) for at in range(slices)]
    for at in range(slices):
        wide_ref[:, at * count : (at + 1) * count] = pieces[at].astype(BF16)
        tall_ref[at * count : (at + 1) * count, :] = pieces[at].T.astype(BF16)
    shape = (slices, count, count)
    on = lax.broadcasted_iota(jnp.int32, shape, 1) == lax.broadcasted_iota(jnp.int32, shape, 2)
    column = jnp.sum(jnp.where(on, thr_ref[...].reshape(1, 1, count), 0.0), axis=2, keepdims=True)
    level[...] = jnp.broadcast_to(column, (slices, count, zp)).reshape(slices * count, zp)

    has_edge = jnp.logical_or(
        jnp.logical_and(q == 0, c > 0), jnp.logical_and(q == last, c < n_c - 1)
    )

    @pl.when(jnp.logical_not(has_edge))
    def _():
        edge[...] = jnp.zeros_like(edge)

    def prepare():
        ext[e, r] = xs_ref[1 + q]
        for d in range(1, peers):
            src = down(d)
            remote(
                xs_ref.at[0], ext.at[src // n_r, lax.rem(src, n_r)], x_send_sem.at[d], x_recv_sem.at[d], (e, c, r)
            ).wait_recv()

        @pl.when(has_edge)
        def _():
            for src in range(peers):
                remote(
                    xs_ref.at[0], edge.at[src // n_r, src % n_r], e_send_sem.at[0], e_recv_sem.at[src], (e, c, r)
                ).wait_recv()

        rows = rq + 4
        taps = 2 * s_local * n_r
        for echo in range(n_e):
            parts = [ext[echo, read].astype(F32) + edge[echo, read].astype(F32) for read in range(n_r)]
            block = jnp.concatenate(parts, axis=1) if n_r > 1 else parts[0]
            flat = block.reshape(rows * taps, zp)
            moved = [
                pltpu.roll(flat, 1, 1).reshape(rows, taps, zp),
                block,
                pltpu.roll(flat, zp - 1, 1).reshape(rows, taps, zp),
            ]
            fill = [jnp.zeros((rows, SLAB - 3 * taps, zp), F32)] if SLAB > 3 * taps else []
            slab[echo] = jnp.concatenate(moved + fill, axis=1).reshape(rows * SLAB, zp).astype(BF16)

        pacc[...] = jnp.zeros_like(pacc)

    def respond(begin, end):
        tall = tall_ref[...]
        wide = wide_ref[...]
        lane_ok = lax.broadcasted_iota(jnp.int32, (1, zp), 1) < nz
        first = c * rb + q * rq - 1

        def row(i, carry):
            start = pl.multiple_of(i * SLAB, SLAB)
            response = [dot(tall, slab[echo, pl.ds(start, 3 * SLAB), :]) for echo in range(n_e)]
            energy = response[0] * response[0]
            for other in response[1:]:
                energy = energy + other * other
            magnitude = jnp.sqrt(energy)
            factor = magnitude / (magnitude + level[...])
            inside = jnp.logical_and(first + i >= 0, first + i < ny)
            factor = jnp.where(jnp.logical_and(lane_ok, inside), factor, 0.0)
            for echo in range(n_e):
                spread = dot(wide, (response[echo] * factor).astype(BF16))
                for a in range(3):
                    pacc[echo, i + a] += spread[a * SLAB : (a + 1) * SLAB]
            return carry

        lax.fori_loop(begin, end, row, 0, unroll=True)

    def collect():
        taps = 2 * s_local * n_r
        for echo in range(n_e):
            held = pacc[echo, 2 : 2 + rq]
            low = pltpu.roll(held[:, :taps].reshape(rq * taps, zp), zp - 1, 1).reshape(rq, taps, zp)
            high = pltpu.roll(held[:, 2 * taps : 3 * taps].reshape(rq * taps, zp), 1, 1).reshape(rq, taps, zp)
            total = low + held[:, taps : 2 * taps] + high
            for read in range(n_r):
                pen_send[echo, read] = total[:, read * 2 * s_local : (read + 1) * 2 * s_local]
        pen_recv[q] = pen_send[e, r]

    def penalty_out(d):
        to = up(d)
        return remote(
            pen_send.at[to // n_r, lax.rem(to, n_r)], pen_recv.at[q], p_send_sem.at[d], p_recv_sem.at[d],
            (to // n_r, c, lax.rem(to, n_r)),
        )

    split = (rq + 2) * 2 // 3

    def before():
        prepare()
        respond(0, split)

    def after():
        respond(split, rq + 2)
        collect()
        for d in range(1, peers):
            penalty_out(d).start()

    when(active(q), before)

    for d in range(1, chips):
        src = lax.rem(c + n_c - 2 * d, n_c)
        remote(img_ref, gat.at[src], ag_send_sem.at[d], ag_recv_sem.at[d], (e, partner, r)).wait_recv()
        forward(d).start()
    remote(img_ref, gat.at[partner], ag_send_sem.at[0], ag_recv_sem.at[0], (e, partner, r)).wait_recv()
    for d in range(1, chips):
        src = lax.rem(partner + n_c - 2 * d, n_c)
        remote(gat.at[src], gat.at[src], f_send_sem.at[d], f_recv_sem.at[d], (e, partner, r)).wait_recv()
    for load in loads:
        load.wait()

    def pair(s):
        return remote(
            part.at[s, :, 1 - core], paired.at[s], pair_send_sem.at[s], pair_recv_sem.at[s], (e, partner, r)
        )

    def scatter(s, d):
        to = lax.rem(chip + d, chips)
        return remote(
            rs_send.at[s, to], rs_recv.at[s, chip], rs_send_sem.at[s, d], rs_recv_sem.at[s, d],
            (e, 2 * to + core, r),
        )

    def send_sums(s):
        pair(s).wait_recv()
        rs_send[s] = (part[s, :, core].astype(F32) + paired[s].astype(F32)).astype(BF16)
        for d in range(1, chips):
            scatter(s, d).start()

    sampled = samp[...].astype(F32)
    for s in range(s_local):
        image = gat[:, :, s * width : (s + 1) * width].astype(F32).reshape(ny, width).T
        real, imag = image[:nz], image[nz:]
        map_real, map_imag = maps[s, 0].astype(F32), maps[s, 1].astype(F32)
        weighted = jnp.concatenate(
            [map_real * real - map_imag * imag, map_real * imag + map_imag * real], 0
        ).astype(BF16)
        halfway = dot(fz[...], weighted).astype(BF16)
        spectrum = dot(halfway, ty[...])
        if s:
            send_sums(s - 1)
        spec_real = spectrum[:nz, :ny] + spectrum[nz:, ny:]
        spec_imag = spectrum[nz:, :ny] - spectrum[:nz, ny:]
        residual = jnp.concatenate(
            [
                sampled * (spec_real - kspace[s, 0].astype(F32)),
                sampled * (spec_imag - kspace[s, 1].astype(F32)),
            ],
            0,
        ).astype(BF16)
        returned = dot(residual, ty[...])
        backward = jnp.concatenate(
            [returned[:nz, :ny] - returned[nz:, ny:], returned[nz:, :ny] + returned[:nz, ny:]], 0
        ).astype(BF16)
        restored = dot(az[...], backward)
        back_real, back_imag = restored[:nz], restored[nz:]
        map_real, map_imag = maps[s, 0].astype(F32), maps[s, 1].astype(F32)
        adjoint = jnp.concatenate(
            [map_real * back_real + map_imag * back_imag, map_real * back_imag - map_imag * back_real], 0
        ).T
        part[s] = adjoint.reshape(chips, 2, rb, width).astype(BF16)
        pair(s).start()
    send_sums(s_local - 1)
    when(active(q), after)

    for d in range(1, peers):
        src = down(d)
        when(
            active(src),
            lambda: remote(
                pen_send.at[0, 0], pen_recv.at[src], p_send_sem.at[d], p_recv_sem.at[d], (e, c, r)
            ).wait_recv(),
        )
    pen_ref[...] = pen_recv[...].reshape(rb, 2 * s_local, zp)

    dc = dc_ref[0]
    for s in range(s_local):
        total = part[s, chip, core].astype(F32) + paired[s, chip].astype(F32)
        for d in range(1, chips):
            src = lax.rem(chip + chips - d, chips)
            remote(
                rs_send.at[s, src], rs_recv.at[s, src], rs_send_sem.at[s, d], rs_recv_sem.at[s, d], (e, partner, r)
            ).wait_recv()
            total = total + rs_recv[s, src].astype(F32)
        adj_ref[:, s * width : (s + 1) * width] = dc * total

    for d in range(chips):
        gather(d).wait_send()
        if d:
            forward(d).wait_send()
            for s in range(s_local):
                scatter(s, d).wait_send()
    for s in range(s_local):
        pair(s).wait_send()
    for d in range(1, peers):
        when(active(up(d)), lambda: window(d).wait_send())
        when(active(q), lambda: penalty_out(d).wait_send())
    pl.when(c < n_c - 1)(lambda: edge_up().wait_send())
    pl.when(c > 0)(lambda: edge_down().wait_send())


def body(kspace, sampling, coil_maps, image, filters, thresholds, dc_weight):
    n_e, n_c, n_r = lax.axis_size("echo"), lax.axis_size("coil"), lax.axis_size("read")
    rb, _, s_local, _, nz = image.shape
    ny = kspace.shape[0]
    peers = n_e * n_r
    rq = window_rows(rb, peers)
    n_q = rb // rq
    zp = -(-(nz + 1) // 128) * 128
    width = 2 * nz
    slices = s_local * n_r
    taps = 2 * slices
    count = filters.shape[0]

    col_cos, col_sin = tables(nz)
    row_cos, row_sin = tables(ny)
    fz = jnp.asarray(np.block([[col_cos, col_sin], [-col_sin, col_cos]]), BF16)
    az = jnp.asarray(np.block([[col_cos, -col_sin], [col_sin, col_cos]]), BF16)
    ty = jnp.asarray(np.concatenate([row_cos, row_sin], 1), BF16)

    rounded = image.astype(BF16)
    flat = rounded.reshape(rb, s_local * width)
    rows = rounded.reshape(rb, 2 * s_local, nz)
    margin = rq + 2
    padded = jnp.pad(rows, ((margin, margin), (0, 0), (0, zp - nz)))
    xs = jnp.stack([padded[j * rq : j * rq + rq + 4] for j in range(n_q + 2)])

    spread = np.zeros((slices, 3, SLAB, 3, 3, 3, 2))
    for at in range(slices):
        for a in range(3):
            for b in range(3):
                for d in range(3):
                    for p in range(2):
                        if 0 <= at + b - 1 < slices:
                            spread[at, a, d * taps + (at + b - 1) * 2 + p, a, b, d, p] = 1.0
    spread = jnp.asarray(spread.reshape(slices, 3 * SLAB, 54), BF16)
    flat_filters = jnp.transpose(filters, (1, 2, 3, 4, 0))
    thr = thresholds[None, :]

    k_view = jnp.transpose(kspace[:, 0, 0], (1, 2, 3, 0))
    m_view = jnp.transpose(coil_maps[:, 0], (1, 2, 3, 0))
    s_view = jnp.transpose(sampling[:, 0], (1, 0))

    k_view, m_view, s_view, fz, az, ty = (
        pltpu.with_memory_space_constraint(x, pltpu.HBM) for x in (k_view, m_view, s_view, fz, az, ty)
    )
    vmem = pl.BlockSpec(memory_space=pltpu.VMEM)
    hbm = pl.BlockSpec(memory_space=pltpu.HBM)
    smem = pl.BlockSpec(memory_space=pltpu.SMEM)
    dma = pltpu.SemaphoreType.DMA
    total, penalty = pl.pallas_call(
        functools.partial(kernel, (n_e, n_c, n_r, n_q, rq, nz, ny)),
        out_shape=(
            jax.ShapeDtypeStruct((rb, s_local * width), F32),
            jax.ShapeDtypeStruct((rb, 2 * s_local, zp), F32),
        ),
        in_specs=[smem, vmem, vmem, hbm, hbm, hbm, hbm, hbm, hbm, vmem, vmem, vmem],
        out_specs=(vmem, vmem),
        scratch_shapes=[
            pltpu.VMEM((n_c, rb, s_local * width), BF16),
            pltpu.VMEM((s_local, n_c // 2, 2, rb, width), BF16),
            pltpu.VMEM((s_local, n_c // 2, rb, width), BF16),
            pltpu.VMEM((s_local, n_c // 2, rb, width), BF16),
            pltpu.VMEM((s_local, n_c // 2, rb, width), BF16),
            pltpu.VMEM((3 * SLAB, slices * count), BF16),
            pltpu.VMEM((slices * count, 3 * SLAB), BF16),
            pltpu.VMEM((slices * count, zp), F32),
            pltpu.VMEM((n_e, n_r, rq + 4, 2 * s_local, zp), BF16),
            pltpu.VMEM((n_e, n_r, rq + 4, 2 * s_local, zp), BF16),
            pltpu.VMEM((n_e, n_r, rq, 2 * s_local, zp), F32),
            pltpu.VMEM((n_q, rq, 2 * s_local, zp), F32),
            pltpu.VMEM((n_e, rq + 4, SLAB, zp), F32),
            pltpu.VMEM((n_e, (rq + 4) * SLAB, zp), BF16),
            pltpu.VMEM(k_view.shape, BF16),
            pltpu.VMEM(m_view.shape, BF16),
            pltpu.VMEM(s_view.shape, jnp.int32),
            pltpu.VMEM(fz.shape, BF16),
            pltpu.VMEM(az.shape, BF16),
            pltpu.VMEM(ty.shape, BF16),
            dma((6,)),
            dma((n_c,)), dma((n_c,)),
            dma((peers,)), dma((peers,)),
            dma((2,)), dma((peers,)),
            dma((peers,)), dma((peers,)),
            dma((s_local, n_c)), dma((s_local, n_c)),
            dma((n_c,)), dma((n_c,)), dma((s_local,)), dma((s_local,)),
        ],
        compiler_params=pltpu.CompilerParams(
            collective_id=0, has_side_effects=True, vmem_limit_bytes=GRANT
        ),
        name="cascade",
    )(dc_weight, flat, xs, k_view, m_view, s_view, fz, az, ty, flat_filters, spread, thr)
    shape = image.shape
    return image - total.reshape(shape) - penalty[:, :, :nz].reshape(shape)


def solution(mesh):
    return jax.shard_map(
        body,
        mesh=mesh,
        in_specs=(
            P(None, "echo", "coil", "read", None, None),
            P(None, "echo", None),
            P(None, "coil", "read", None, None),
            P("coil", "echo", "read", None, None),
            P(),
            P(),
            P("echo"),
        ),
        out_specs=P("coil", "echo", "read", None, None),
        check_vma=False,
    )
```

```python
import functools

import numpy as np
import jax
import jax.numpy as jnp
from jax import lax
from jax.experimental import pallas as pl
from jax.experimental.pallas import tpu as pltpu
from jax.sharding import PartitionSpec as P

MESH = pl.DeviceIdType.MESH
F32 = jnp.float32
BF16 = jnp.bfloat16
SLAB = 32
GRANT = 24 << 20


def tables(length):
    product = np.outer(np.arange(length), np.arange(length)) % length
    phases = product * (2.0 * np.pi / length)
    normalize = length ** (-0.5)
    return np.cos(phases) * normalize, np.sin(phases) * normalize


def window_rows(rows, peers):
    for size in range(2, rows + 1):
        if rows % size == 0 and rows // size <= peers:
            return size
    return rows


def dot(left, right):
    return jnp.dot(left, right, preferred_element_type=F32)


def kernel(
    cfg,
    dc_ref, img_ref, xs_ref, kspace_hbm, maps_hbm, samp_hbm, fz_hbm, az_hbm, ty_hbm,
    filters_ref, spread_hbm, thr_ref,
    adj_ref, pen_ref,
    gat, part, paired, rs_send, rs_recv, wide_ref, tall_ref, level, ext, edge, pen_send, pen_recv, pacc, slab,
    kspace, maps, samp, fz, az, ty, spread,
    local_sem, ag_send_sem, ag_recv_sem, x_send_sem, x_recv_sem, e_send_sem, e_recv_sem,
    p_send_sem, p_recv_sem, rs_send_sem, rs_recv_sem, f_send_sem, f_recv_sem, pair_send_sem, pair_recv_sem,
):
    n_e, n_c, n_r, n_q, rq, nz, ny = cfg
    peers = n_e * n_r
    e = lax.axis_index("echo")
    c = lax.axis_index("coil")
    r = lax.axis_index("read")
    q = e * n_r + r
    s_local, rb = rs_send.shape[0], img_ref.shape[0]
    chips = n_c // 2
    core = lax.rem(c, 2)
    chip = c // 2
    partner = c + 1 - 2 * core
    width = 2 * nz
    zp = ext.shape[-1]

    loads = [
        pltpu.make_async_copy(src, dst, local_sem.at[i])
        for i, (src, dst) in enumerate(
            [(spread_hbm, spread), (kspace_hbm, kspace), (maps_hbm, maps), (samp_hbm, samp), (fz_hbm, fz), (az_hbm, az), (ty_hbm, ty)]
        )
    ]

    for load in loads:
        load.start()

    def remote(src, dst, send, recv, target):
        return pltpu.make_async_remote_copy(
            src_ref=src, dst_ref=dst, send_sem=send, recv_sem=recv, device_id=target, device_id_type=MESH
        )

    def when(condition, act):
        if condition is True:
            act()
        else:
            pl.when(condition)(act)

    def up(d):
        return lax.rem(q + d, peers)

    def down(d):
        return lax.rem(q + peers - d, peers)

    def active(which):
        return True if n_q == peers else which < n_q

    barrier = pltpu.get_barrier_semaphore()
    for d in range(chips):
        to = lax.rem(c + 2 * d, n_c) if d else partner
        pl.semaphore_signal(barrier, inc=1, device_id=(e, to, r), device_id_type=MESH)
    for d in range(peers):
        if d:
            pl.semaphore_signal(barrier, inc=1, device_id=(up(d) // n_r, c, lax.rem(up(d), n_r)), device_id_type=MESH)
        for step, ok in ((1, c < n_c - 1), (-1, c > 0)):
            @pl.when(ok)
            def _():
                pl.semaphore_signal(
                    barrier, inc=1, device_id=(up(d) // n_r, c + step, lax.rem(up(d), n_r)), device_id_type=MESH
                )
    sides = jnp.minimum(c, 1) + jnp.minimum(n_c - 1 - c, 1)
    pl.semaphore_wait(barrier, chips + peers - 1 + peers * sides)

    def window(d):
        to = up(d)
        return remote(
            xs_ref.at[1 + to], ext.at[e, r], x_send_sem.at[d], x_recv_sem.at[d], (to // n_r, c, lax.rem(to, n_r))
        )

    last = n_q - 1
    edge_up = lambda: remote(
        xs_ref.at[n_q + 1], edge.at[e, r], e_send_sem.at[0], e_recv_sem.at[q], (0, c + 1, 0)
    )
    edge_down = lambda: remote(
        xs_ref.at[0], edge.at[e, r], e_send_sem.at[1], e_recv_sem.at[q], (last // n_r, c - 1, last % n_r)
    )
    for d in range(1, peers):
        when(active(up(d)), lambda: window(d).start())
    pl.when(c < n_c - 1)(lambda: edge_up().start())
    pl.when(c > 0)(lambda: edge_down().start())

    def gather(d):
        to = lax.rem(c + 2 * d, n_c) if d else partner
        return remote(img_ref, gat.at[c], ag_send_sem.at[d], ag_recv_sem.at[d], (e, to, r))

    def forward(d):
        src = lax.rem(c + n_c - 2 * d, n_c)
        return remote(gat.at[src], gat.at[src], f_send_sem.at[d], f_recv_sem.at[d], (e, partner, r))

    for d in range(chips):
        gather(d).start()
    gat[c] = img_ref[...]

    count = filters_ref.shape[-1]
    slices = s_local * n_r
    flat_filters = filters_ref[...].astype(F32).reshape(-1, count).astype(BF16)
    loads[0].wait()
    pieces = [dot(spread[at], flat_filters) for at in range(slices)]
    for at in range(slices):
        wide_ref[:, at * count : (at + 1) * count] = pieces[at].astype(BF16)
        tall_ref[at * count : (at + 1) * count, :] = pieces[at].T.astype(BF16)
    shape = (slices, count, count)
    on = lax.broadcasted_iota(jnp.int32, shape, 1) == lax.broadcasted_iota(jnp.int32, shape, 2)
    column = jnp.sum(jnp.where(on, thr_ref[...].reshape(1, 1, count), 0.0), axis=2, keepdims=True)
    level[...] = jnp.broadcast_to(column, (slices, count, zp)).reshape(slices * count, zp)

    has_edge = jnp.logical_or(
        jnp.logical_and(q == 0, c > 0), jnp.logical_and(q == last, c < n_c - 1)
    )

    @pl.when(jnp.logical_not(has_edge))
    def _():
        edge[...] = jnp.zeros_like(edge)

    def prepare():
        ext[e, r] = xs_ref[1 + q]
        for d in range(1, peers):
            src = down(d)
            remote(
                xs_ref.at[0], ext.at[src // n_r, lax.rem(src, n_r)], x_send_sem.at[d], x_recv_sem.at[d], (e, c, r)
            ).wait_recv()

        @pl.when(has_edge)
        def _():
            for src in range(peers):
                remote(
                    xs_ref.at[0], edge.at[src // n_r, src % n_r], e_send_sem.at[0], e_recv_sem.at[src], (e, c, r)
                ).wait_recv()

        rows = rq + 4
        taps = 2 * s_local * n_r
        for echo in range(n_e):
            parts = [ext[echo, read].astype(F32) + edge[echo, read].astype(F32) for read in range(n_r)]
            block = jnp.concatenate(parts, axis=1) if n_r > 1 else parts[0]
            flat = block.reshape(rows * taps, zp)
            moved = [
                pltpu.roll(flat, 1, 1).reshape(rows, taps, zp),
                block,
                pltpu.roll(flat, zp - 1, 1).reshape(rows, taps, zp),
            ]
            fill = [jnp.zeros((rows, SLAB - 3 * taps, zp), F32)] if SLAB > 3 * taps else []
            slab[echo] = jnp.concatenate(moved + fill, axis=1).reshape(rows * SLAB, zp).astype(BF16)

        pacc[...] = jnp.zeros_like(pacc)

    def respond(begin, end):
        tall = tall_ref[...]
        wide = wide_ref[...]
        lane_ok = lax.broadcasted_iota(jnp.int32, (1, zp), 1) < nz
        first = c * rb + q * rq - 1

        def row(i, carry):
            start = pl.multiple_of(i * SLAB, SLAB)
            response = [dot(tall, slab[echo, pl.ds(start, 3 * SLAB), :]) for echo in range(n_e)]
            energy = response[0] * response[0]
            for other in response[1:]:
                energy = energy + other * other
            magnitude = jnp.sqrt(energy)
            factor = magnitude / (magnitude + level[...])
            inside = jnp.logical_and(first + i >= 0, first + i < ny)
            factor = jnp.where(jnp.logical_and(lane_ok, inside), factor, 0.0)
            for echo in range(n_e):
                spread = dot(wide, (response[echo] * factor).astype(BF16))
                for a in range(3):
                    pacc[echo, i + a] += spread[a * SLAB : (a + 1) * SLAB]
            return carry

        lax.fori_loop(begin, end, row, 0, unroll=True)

    def collect():
        taps = 2 * s_local * n_r
        for echo in range(n_e):
            held = pacc[echo, 2 : 2 + rq]
            low = pltpu.roll(held[:, :taps].reshape(rq * taps, zp), zp - 1, 1).reshape(rq, taps, zp)
            high = pltpu.roll(held[:, 2 * taps : 3 * taps].reshape(rq * taps, zp), 1, 1).reshape(rq, taps, zp)
            total = low + held[:, taps : 2 * taps] + high
            for read in range(n_r):
                pen_send[echo, read] = total[:, read * 2 * s_local : (read + 1) * 2 * s_local]
        pen_recv[q] = pen_send[e, r]

    def penalty_out(d):
        to = up(d)
        return remote(
            pen_send.at[to // n_r, lax.rem(to, n_r)], pen_recv.at[q], p_send_sem.at[d], p_recv_sem.at[d],
            (to // n_r, c, lax.rem(to, n_r)),
        )

    split = (rq + 2) * 2 // 3

    def before():
        prepare()
        respond(0, split)

    def after():
        respond(split, rq + 2)
        collect()
        for d in range(1, peers):
            penalty_out(d).start()

    when(active(q), before)

    for d in range(1, chips):
        src = lax.rem(c + n_c - 2 * d, n_c)
        remote(img_ref, gat.at[src], ag_send_sem.at[d], ag_recv_sem.at[d], (e, partner, r)).wait_recv()
        forward(d).start()
    remote(img_ref, gat.at[partner], ag_send_sem.at[0], ag_recv_sem.at[0], (e, partner, r)).wait_recv()
    for d in range(1, chips):
        src = lax.rem(partner + n_c - 2 * d, n_c)
        remote(gat.at[src], gat.at[src], f_send_sem.at[d], f_recv_sem.at[d], (e, partner, r)).wait_recv()
    for load in loads[1:]:
        load.wait()

    def pair(s):
        return remote(
            part.at[s, :, 1 - core], paired.at[s], pair_send_sem.at[s], pair_recv_sem.at[s], (e, partner, r)
        )

    def scatter(s, d):
        to = lax.rem(chip + d, chips)
        return remote(
            rs_send.at[s, to], rs_recv.at[s, chip], rs_send_sem.at[s, d], rs_recv_sem.at[s, d],
            (e, 2 * to + core, r),
        )

    def send_sums(s):
        pair(s).wait_recv()
        rs_send[s] = (part[s, :, core].astype(F32) + paired[s].astype(F32)).astype(BF16)
        for d in range(1, chips):
            scatter(s, d).start()

    sampled = samp[...].astype(F32)
    for s in range(s_local):
        image = gat[:, :, s * width : (s + 1) * width].astype(F32).reshape(ny, width).T
        real, imag = image[:nz], image[nz:]
        map_real, map_imag = maps[s, 0].astype(F32), maps[s, 1].astype(F32)
        weighted = jnp.concatenate(
            [map_real * real - map_imag * imag, map_real * imag + map_imag * real], 0
        ).astype(BF16)
        halfway = dot(fz[...], weighted).astype(BF16)
        spectrum = dot(halfway, ty[...])
        if s:
            send_sums(s - 1)
        spec_real = spectrum[:nz, :ny] + spectrum[nz:, ny:]
        spec_imag = spectrum[nz:, :ny] - spectrum[:nz, ny:]
        residual = jnp.concatenate(
            [
                sampled * (spec_real - kspace[s, 0].astype(F32)),
                sampled * (spec_imag - kspace[s, 1].astype(F32)),
            ],
            0,
        ).astype(BF16)
        returned = dot(residual, ty[...])
        backward = jnp.concatenate(
            [returned[:nz, :ny] - returned[nz:, ny:], returned[nz:, :ny] + returned[:nz, ny:]], 0
        ).astype(BF16)
        restored = dot(az[...], backward)
        back_real, back_imag = restored[:nz], restored[nz:]
        map_real, map_imag = maps[s, 0].astype(F32), maps[s, 1].astype(F32)
        adjoint = jnp.concatenate(
            [map_real * back_real + map_imag * back_imag, map_real * back_imag - map_imag * back_real], 0
        ).T
        part[s] = adjoint.reshape(chips, 2, rb, width).astype(BF16)
        pair(s).start()
    send_sums(s_local - 1)
    when(active(q), after)

    for d in range(1, peers):
        src = down(d)
        when(
            active(src),
            lambda: remote(
                pen_send.at[0, 0], pen_recv.at[src], p_send_sem.at[d], p_recv_sem.at[d], (e, c, r)
            ).wait_recv(),
        )
    pen_ref[...] = pen_recv[...].reshape(rb, 2 * s_local, zp)

    dc = dc_ref[0]
    for s in range(s_local):
        total = part[s, chip, core].astype(F32) + paired[s, chip].astype(F32)
        for d in range(1, chips):
            src = lax.rem(chip + chips - d, chips)
            remote(
                rs_send.at[s, src], rs_recv.at[s, src], rs_send_sem.at[s, d], rs_recv_sem.at[s, d], (e, partner, r)
            ).wait_recv()
            total = total + rs_recv[s, src].astype(F32)
        adj_ref[:, s * width : (s + 1) * width] = dc * total

    for d in range(chips):
        gather(d).wait_send()
        if d:
            forward(d).wait_send()
            for s in range(s_local):
                scatter(s, d).wait_send()
    for s in range(s_local):
        pair(s).wait_send()
    for d in range(1, peers):
        when(active(up(d)), lambda: window(d).wait_send())
        when(active(q), lambda: penalty_out(d).wait_send())
    pl.when(c < n_c - 1)(lambda: edge_up().wait_send())
    pl.when(c > 0)(lambda: edge_down().wait_send())


def body(kspace, sampling, coil_maps, image, filters, thresholds, dc_weight):
    n_e, n_c, n_r = lax.axis_size("echo"), lax.axis_size("coil"), lax.axis_size("read")
    rb, _, s_local, _, nz = image.shape
    ny = kspace.shape[0]
    peers = n_e * n_r
    rq = window_rows(rb, peers)
    n_q = rb // rq
    zp = -(-(nz + 1) // 128) * 128
    width = 2 * nz
    slices = s_local * n_r
    taps = 2 * slices
    count = filters.shape[0]

    col_cos, col_sin = tables(nz)
    row_cos, row_sin = tables(ny)
    fz = jnp.asarray(np.block([[col_cos, col_sin], [-col_sin, col_cos]]), BF16)
    az = jnp.asarray(np.block([[col_cos, -col_sin], [col_sin, col_cos]]), BF16)
    ty = jnp.asarray(np.concatenate([row_cos, row_sin], 1), BF16)

    rounded = image.astype(BF16)
    flat = rounded.reshape(rb, s_local * width)
    rows = rounded.reshape(rb, 2 * s_local, nz)
    margin = rq + 2
    padded = jnp.pad(rows, ((margin, margin), (0, 0), (0, zp - nz)))
    xs = jnp.stack([padded[j * rq : j * rq + rq + 4] for j in range(n_q + 2)])

    spread = np.zeros((slices, 3, SLAB, 3, 3, 3, 2))
    for at in range(slices):
        for a in range(3):
            for b in range(3):
                for d in range(3):
                    for p in range(2):
                        if 0 <= at + b - 1 < slices:
                            spread[at, a, d * taps + (at + b - 1) * 2 + p, a, b, d, p] = 1.0
    spread = jnp.asarray(spread.reshape(slices, 3 * SLAB, 54), BF16)
    flat_filters = jnp.transpose(filters, (1, 2, 3, 4, 0))
    thr = thresholds[None, :]

    k_view = jnp.transpose(kspace[:, 0, 0], (1, 2, 3, 0))
    m_view = jnp.transpose(coil_maps[:, 0], (1, 2, 3, 0))
    s_view = jnp.transpose(sampling[:, 0], (1, 0))

    k_view, m_view, s_view, fz, az, ty, spread = (
        pltpu.with_memory_space_constraint(x, pltpu.HBM) for x in (k_view, m_view, s_view, fz, az, ty, spread)
    )
    vmem = pl.BlockSpec(memory_space=pltpu.VMEM)
    hbm = pl.BlockSpec(memory_space=pltpu.HBM)
    smem = pl.BlockSpec(memory_space=pltpu.SMEM)
    dma = pltpu.SemaphoreType.DMA
    total, penalty = pl.pallas_call(
        functools.partial(kernel, (n_e, n_c, n_r, n_q, rq, nz, ny)),
        out_shape=(
            jax.ShapeDtypeStruct((rb, s_local * width), F32),
            jax.ShapeDtypeStruct((rb, 2 * s_local, zp), F32),
        ),
        in_specs=[smem, vmem, vmem, hbm, hbm, hbm, hbm, hbm, hbm, vmem, hbm, vmem],
        out_specs=(vmem, vmem),
        scratch_shapes=[
            pltpu.VMEM((n_c, rb, s_local * width), BF16),
            pltpu.VMEM((s_local, n_c // 2, 2, rb, width), BF16),
            pltpu.VMEM((s_local, n_c // 2, rb, width), BF16),
            pltpu.VMEM((s_local, n_c // 2, rb, width), BF16),
            pltpu.VMEM((s_local, n_c // 2, rb, width), BF16),
            pltpu.VMEM((3 * SLAB, slices * count), BF16),
            pltpu.VMEM((slices * count, 3 * SLAB), BF16),
            pltpu.VMEM((slices * count, zp), F32),
            pltpu.VMEM((n_e, n_r, rq + 4, 2 * s_local, zp), BF16),
            pltpu.VMEM((n_e, n_r, rq + 4, 2 * s_local, zp), BF16),
            pltpu.VMEM((n_e, n_r, rq, 2 * s_local, zp), F32),
            pltpu.VMEM((n_q, rq, 2 * s_local, zp), F32),
            pltpu.VMEM((n_e, rq + 4, SLAB, zp), F32),
            pltpu.VMEM((n_e, (rq + 4) * SLAB, zp), BF16),
            pltpu.VMEM(k_view.shape, BF16),
            pltpu.VMEM(m_view.shape, BF16),
            pltpu.VMEM(s_view.shape, jnp.int32),
            pltpu.VMEM(fz.shape, BF16),
            pltpu.VMEM(az.shape, BF16),
            pltpu.VMEM(ty.shape, BF16),
            pltpu.VMEM(spread.shape, BF16),
            dma((7,)),
            dma((n_c,)), dma((n_c,)),
            dma((peers,)), dma((peers,)),
            dma((2,)), dma((peers,)),
            dma((peers,)), dma((peers,)),
            dma((s_local, n_c)), dma((s_local, n_c)),
            dma((n_c,)), dma((n_c,)), dma((s_local,)), dma((s_local,)),
        ],
        compiler_params=pltpu.CompilerParams(
            collective_id=0, has_side_effects=True, vmem_limit_bytes=GRANT
        ),
        name="cascade",
    )(dc_weight, flat, xs, k_view, m_view, s_view, fz, az, ty, flat_filters, spread, thr)
    shape = image.shape
    return image - total.reshape(shape) - penalty[:, :, :nz].reshape(shape)


def solution(mesh):
    return jax.shard_map(
        body,
        mesh=mesh,
        in_specs=(
            P(None, "echo", "coil", "read", None, None),
            P(None, "echo", None),
            P(None, "coil", "read", None, None),
            P("coil", "echo", "read", None, None),
            P(),
            P(),
            P("echo"),
        ),
        out_specs=P("coil", "echo", "read", None, None),
        check_vma=False,
    )
```
